128 devices in a mesh: ctx: 16 (over x, z), head: 8 (over y, core).
Axes of the slice: x: 4, y: 4, z: 4, core: 2. Of those that a mesh axis runs over, the one named last changes fastest.
Arguments:
- queries: bfloat16 [64, 8192], P('ctx', 'head'), may hold values from -16 to 16
- keys: bfloat16 [524288, 8, 128], P('ctx', 'head'), may hold values from -16 to 16
- values: bfloat16 [524288, 8, 128], P('ctx', 'head'), may hold values from -4 to 4
- offsets: int32 [16], P('ctx'), may hold values from 0 to 491520, as said below
- lengths: int32 [64], replicated, may hold values from 262144 to 524288
- residual: bfloat16 [64, 5120], P(None, 'ctx'), may hold values from -2 to 2
- wo: bfloat16 [8192, 5120], P('head', 'ctx'), may hold values from -0.0625 to 0.0625
- norm_gain: float32 [5120], P('ctx'), may hold values from 0.1 to 1.9
- w_gate: bfloat16 [5120, 25600], P('ctx', 'head'), may hold values from -0.078125 to 0.078125
- w_up: bfloat16 [5120, 25600], P('ctx', 'head'), may hold values from -0.078125 to 0.078125
- w_down: bfloat16 [25600, 5120], P('head', 'ctx'), may hold values from -0.0390625 to 0.0390625
Outputs:
- attended: bfloat16 [64, 8192], P('ctx', 'head')
- stream: bfloat16 [64, 5120], P(None, 'ctx')
- ffn_out: bfloat16 [64, 5120], P('head', 'ctx')
The draws below stay inside these ranges and needn't reach their ends.
Inputs may be any that keep to these rules, and one draw needn't show every extreme that they name: offsets holds each of 0, 32768, ..., 491520 once.
All inputs are finite; a program needn't handle non-finite values.
Results may differ from the reference program's by a relative error of at most 0.02.
Values may be sent and summed in bfloat16 or wider, within the bound.
A program may use at most 128 MiB of HBM per device.

```python
import math
import jax
import jax.numpy as jnp
from jax import lax

D = 5120
HQ = 64
KVH = 8
HD = 128
FF = 25600
B = 64
CTX_DEV = 32768
SEQ = 524288
SHARDS = 16


def shard_order(key):
    return jax.random.permutation(jax.random.fold_in(key, 31), SHARDS).astype(jnp.int32)


def draw_offsets(key, part):
    return shard_order(key) * CTX_DEV


def draw_queries(key, part):
    noise_key = jax.random.fold_in(key, 1)
    field = jax.random.normal(noise_key, (B, HQ, HD), jnp.float32)
    return jnp.clip(field, -16.0, 16.0).reshape(B, HQ * HD).astype(jnp.bfloat16)


def draw_keys(key, part):
    noise_key = jax.random.fold_in(key, 2)
    field = 2.5 * jax.random.normal(noise_key, (SEQ, KVH, HD), jnp.float32)
    return jnp.clip(field, -15.0, 15.0).astype(jnp.bfloat16)


def draw_values(key, part):
    noise_key, level_key = jax.random.split(jax.random.fold_in(key, 3))
    levels = jax.random.normal(level_key, (2 * SHARDS, KVH, HD), jnp.float32)
    levels = jnp.repeat(levels, CTX_DEV // 2, axis=0)
    noise = 0.3 * jax.random.normal(noise_key, (SEQ, KVH, HD), jnp.float32)
    return jnp.clip(noise + 0.6 * levels, -4.0, 4.0).astype(jnp.bfloat16)


def draw_residual(key, part):
    column_key, row_key, noise_key = jax.random.split(jax.random.fold_in(key, 5), 3)
    ramp = jnp.exp(jnp.linspace(0.0, math.log(3.0), D)) / math.sqrt(3.0)
    columns = ramp * 10.0 ** jax.random.uniform(column_key, (D,), jnp.float32, -0.5, 0.5)
    rows = 10.0 ** jax.random.uniform(row_key, (B, 1), jnp.float32, -0.5, 0.5)
    noise = jax.random.normal(noise_key, (B, D), jnp.float32)
    return jnp.clip(0.15 * rows * columns * noise, -2.0, 2.0).astype(jnp.bfloat16)


def place_ends(values, own_key, smallest, top_value):
    longest = values.shape.index(max(values.shape))
    spots = []
    for shift in (0, 1):
        where = [jax.random.randint(jax.random.fold_in(own_key, axis), (), 0, length) for axis, length in enumerate(values.shape)]
        where[longest] = (where[longest] + shift) % values.shape[longest]
        spots.append(tuple(where))
    return values.at[spots[0]].set(smallest).at[spots[1]].set(top_value)


def shard_levels(stream_key, shape, cuts, low, high):
    def one(axis_at, parts):
        steps = jax.random.uniform(jax.random.fold_in(jax.random.fold_in(stream_key, 6), axis_at), (parts,), jnp.float32, low / len(cuts), high / len(cuts))
        return jnp.repeat(jnp.exp(steps), shape[axis_at] // parts).reshape((-1,) + (1,) * (len(shape) - axis_at - 1))

    level = one(*cuts[0])
    for cut in cuts[1:]:
        level = level * one(*cut)
    return level


def normal_values(key, extent, width, most, pieces=(), kind=jnp.bfloat16):
    values = jax.random.normal(key, extent, jnp.float32) * width
    if len(pieces) > 0:
        values = shard_levels(key, extent, pieces, -0.22, 0.18) * values
    return jnp.clip(values, min=-most, max=most).astype(kind)


def setup_inputs(seed: int = 0) -> dict:
    streams_of = jax.random.split(jax.random.key(seed), 12)
    queries = draw_queries(jax.random.fold_in(streams_of[11], 71), 0)
    keys = draw_keys(jax.random.fold_in(streams_of[11], 71), 0)
    values = draw_values(jax.random.fold_in(streams_of[11], 71), 0)
    offsets = draw_offsets(jax.random.fold_in(streams_of[11], 71), 0)
    lengths = place_ends(jax.random.randint(streams_of[4], (B,), SEQ // 2, SEQ + 1), jax.random.fold_in(streams_of[4], 1), SEQ // 2, SEQ).astype(jnp.int32)
    residual = draw_residual(jax.random.fold_in(streams_of[11], 71), 0)
    wo = normal_values(streams_of[6], (HQ * HD, D), (HQ * HD) ** -0.5, 0.0625, ((0, 8), (1, 16)))
    norm_gain = jnp.clip(1.0 + 0.18 * jax.random.normal(streams_of[7], (D,), jnp.float32), 0.1, 1.9)
    w_gate = normal_values(streams_of[8], (D, FF), D ** -0.5, 0.078125, ((0, 16), (1, 8)))
    w_up = normal_values(streams_of[9], (D, FF), D ** -0.5, 0.078125, ((0, 16), (1, 8)))
    w_down = normal_values(streams_of[10], (FF, D), FF ** -0.5, 0.0390625, ((0, 8), (1, 16)))
    return {"queries": queries, "keys": keys, "values": values, "offsets": offsets, "lengths": lengths, "residual": residual, "wo": wo, "norm_gain": norm_gain, "w_gate": w_gate, "w_up": w_up, "w_down": w_down}


masked_score = -1e+30
epsilon = 1e-06

def reference(queries, keys, values, offsets, lengths, residual, wo, norm_gain, w_gate, w_up, w_down):
    groups = HQ // KVH
    query_heads = queries.astype(jnp.float32).reshape(B, KVH, groups, HD)
    query_heads = query_heads.transpose(1, 0, 2, 3).reshape(KVH, B * groups, HD)
    row_limit = jnp.repeat(lengths, groups)
    inverse_root = 1.0 / math.sqrt(HD)

    def visit(carry, shard_index):
        row_high, row_total, row_acc = carry
        first_slot = (shard_index * CTX_DEV).astype(jnp.int32)
        key_block = lax.dynamic_slice_in_dim(keys, first_slot, CTX_DEV, 0).astype(jnp.float32)
        value_block = lax.dynamic_slice_in_dim(values, first_slot, CTX_DEV, 0).astype(jnp.float32)
        scores = jnp.einsum('hrd,khd->hrk', query_heads, key_block) * inverse_root
        position = offsets[shard_index] + jnp.arange(CTX_DEV, dtype=jnp.int32)
        scores = jnp.where(position[None, None, :] < row_limit[None, :, None], scores, masked_score)
        new_high = jnp.maximum(row_high, lax.optimization_barrier(jnp.max(scores, axis=2)))
        weights = jnp.exp(scores - new_high[:, :, None])
        rounded = lax.optimization_barrier(weights.astype(jnp.bfloat16)).astype(jnp.float32)
        rescale = jnp.exp(row_high - new_high)
        row_total = row_total * rescale + lax.optimization_barrier(jnp.sum(weights, axis=2))
        row_acc = row_acc * rescale[:, :, None] + jnp.einsum('hrk,khd->hrd', rounded, value_block)
        return ((new_high, row_total, row_acc), None)
    start_high = jnp.full((KVH, B * groups), masked_score, jnp.float32)
    start_total = jnp.zeros((KVH, B * groups), jnp.float32)
    start_acc = jnp.zeros((KVH, B * groups, HD), jnp.float32)
    (row_high, row_total, row_acc), _ = lax.scan(visit, (start_high, start_total, start_acc), jnp.arange(SHARDS, dtype=jnp.int32))
    merged = row_acc / row_total[:, :, None]
    merged = merged.reshape(KVH, B, groups, HD).transpose(1, 0, 2, 3).reshape(B, HQ * HD)
    attended = merged.astype(jnp.bfloat16)
    projected = jnp.dot(attended, wo, preferred_element_type=jnp.float32)
    combined = residual.astype(jnp.float32) + projected
    stream = combined.astype(jnp.bfloat16)
    scale = lax.rsqrt(lax.optimization_barrier(jnp.sum(combined * combined, axis=1)) / D + epsilon)[:, None]
    normed = (combined * norm_gain).astype(jnp.bfloat16)
    gate = scale * jnp.dot(normed, w_gate, preferred_element_type=jnp.float32)
    upward = scale * jnp.dot(normed, w_up, preferred_element_type=jnp.float32)
    hidden = (jax.nn.silu(gate) * upward).astype(jnp.bfloat16)
    ffn_out = jnp.dot(hidden, w_down, preferred_element_type=jnp.float32).astype(jnp.bfloat16)
    return (attended, stream, ffn_out)
```

```python
import functools
import math

import jax
import jax.numpy as jnp
from jax import lax
from jax.experimental import pallas as pl
from jax.experimental.pallas import tpu as pltpu
from jax.sharding import PartitionSpec as P

MESH = pl.DeviceIdType.MESH
F32 = jnp.float32
BF16 = jnp.bfloat16
EPSILON = 1e-06
HIDDEN_SCORE = -1e30
GROUPS = 8
HEAD = 128
LANES = 128


def dot(a, b):
    return jnp.dot(a, b, preferred_element_type=F32)


def dot_across(a, b):
    return lax.dot_general(a, b, (((1,), (1,)), ((), ())), preferred_element_type=F32)


def kernel(
    sizes,
    queries,
    lengths,
    offsets,
    residual,
    gain,
    keys,
    values,
    wo,
    w_gate,
    w_up,
    w_down,
    attended,
    stream,
    ffn_out,
    key_buf,
    value_buf,
    wo_buf,
    pair_buf,
    down_buf,
    visible,
    query_row,
    query_send,
    query_all,
    query_wide,
    score_buf,
    high,
    total,
    acc,
    part_send,
    part_recv,
    rows_f32,
    rows_send,
    rows_all,
    wide_f32,
    proj_all,
    square_tile,
    lhs,
    gate_send,
    gate_recv,
    hidden_send,
    hidden_all,
    down_send,
    down_recv,
    load_sem,
    weight_sem,
    ctx_send,
    ctx_recv,
    head_send,
    head_recv,
):
    ctxs, heads, span, block, width, model = sizes
    batch = 4 * ctxs
    rows = batch * GROUPS
    turns = span // block
    hidden_width = w_gate.shape[1]
    first = pair_buf.shape[1]
    second = hidden_width - first
    base = 1.0 / math.sqrt(HEAD) * math.log2(math.e)
    ctx = lax.axis_index("ctx")
    head = lax.axis_index("head")

    def key_copy(c):
        part = pl.ds(pl.multiple_of(c * block, block), block)
        return pltpu.make_async_copy(keys.at[part], key_buf.at[part], load_sem.at[0, c])

    def value_copy(c):
        part = pl.ds(pl.multiple_of(c * block, block), block)
        return pltpu.make_async_copy(values.at[part], value_buf.at[part], load_sem.at[1, c])

    weight_copies = [
        pltpu.make_async_copy(wo, wo_buf, weight_sem.at[0]),
        pltpu.make_async_copy(
            w_gate.at[:, 0:first], pair_buf.at[0:width, :], weight_sem.at[1]
        ),
        pltpu.make_async_copy(
            w_up.at[:, 0:first], pair_buf.at[width : 2 * width, :], weight_sem.at[2]
        ),
        pltpu.make_async_copy(
            w_gate.at[:, first:hidden_width],
            pair_buf.at[2 * width : 3 * width, 0:second],
            weight_sem.at[3],
        ),
        pltpu.make_async_copy(
            w_up.at[:, first:hidden_width],
            pair_buf.at[3 * width : 4 * width, 0:second],
            weight_sem.at[4],
        ),
        pltpu.make_async_copy(w_down, down_buf, weight_sem.at[5]),
    ]

    barrier = pltpu.get_barrier_semaphore()

    def greet_ctx(p, _):
        pl.semaphore_signal(
            barrier, inc=1, device_id={"ctx": lax.rem(ctx + p, ctxs)}, device_id_type=MESH
        )
        return 0

    def greet_head(p, _):
        pl.semaphore_signal(
            barrier, inc=1, device_id={"head": lax.rem(head + p, heads)}, device_id_type=MESH
        )
        return 0

    lax.fori_loop(1, ctxs, greet_ctx, 0)
    lax.fori_loop(1, heads, greet_head, 0)

    def fetch(c, _):
        key_copy(c).start()
        value_copy(c).start()
        return 0

    lax.fori_loop(0, turns, fetch, 0)
    for copy in weight_copies:
        copy.start()

    def over_ctx(phase, source, slots):
        def one(other, mine):
            return pltpu.make_async_remote_copy(
                src_ref=source(other),
                dst_ref=slots.at[mine],
                send_sem=ctx_send.at[phase, other],
                recv_sem=ctx_recv.at[phase, mine],
                device_id={"ctx": other},
                device_id_type=MESH,
            )

        def start(p, _):
            one(lax.rem(ctx + p, ctxs), ctx).start()
            return 0

        def arrive(p, _):
            other = lax.rem(ctx + ctxs - p, ctxs)
            one(other, other).wait_recv()
            return 0

        def sent(p, _):
            one(lax.rem(ctx + p, ctxs), ctx).wait_send()
            return 0

        return (
            lambda: lax.fori_loop(1, ctxs, start, 0),
            lambda: lax.fori_loop(1, ctxs, arrive, 0),
            lambda: lax.fori_loop(1, ctxs, sent, 0),
        )

    def over_head(phase, source, slots):
        def one(other, mine):
            return pltpu.make_async_remote_copy(
                src_ref=source(other),
                dst_ref=slots.at[mine],
                send_sem=head_send.at[phase, other],
                recv_sem=head_recv.at[phase, mine],
                device_id={"head": other},
                device_id_type=MESH,
            )

        def start(p, _):
            one(lax.rem(head + p, heads), head).start()
            return 0

        def arrive(p, _):
            other = lax.rem(head + heads - p, heads)
            one(other, other).wait_recv()
            return 0

        def sent(p, _):
            one(lax.rem(head + p, heads), head).wait_send()
            return 0

        return (
            lambda: lax.fori_loop(1, heads, start, 0),
            lambda: lax.fori_loop(1, heads, arrive, 0),
            lambda: lax.fori_loop(1, heads, sent, 0),
        )

    own = queries[...].astype(F32)
    for g in range(GROUPS):
        query_row[pl.ds(g, 4, stride=GROUPS), :] = own[:, g * HEAD : (g + 1) * HEAD]
    query_send[...] = query_row[...].astype(BF16)
    query_all[ctx] = query_send[...]

    pl.semaphore_wait(barrier, ctxs - 1 + heads - 1)
    q_start, q_arrive, q_sent = over_ctx(0, lambda other: query_send, query_all)
    q_start()

    visible[...] = jnp.full(visible.shape, 2**30, jnp.int32)
    visible[0:1, 0:batch] = lengths[...] - offsets[0]
    high[...] = jnp.full(high.shape, -3e38, F32)
    total[...] = jnp.zeros(total.shape, F32)
    acc[...] = jnp.zeros(acc.shape, F32)
    row_of = lax.broadcasted_iota(jnp.int32, (rows, LANES), 0) // GROUPS
    column = lax.broadcasted_iota(jnp.int32, (rows, LANES), 1)
    query_wide[:, HEAD : HEAD + LANES] = jnp.where(row_of == column, HIDDEN_SCORE, 0.0).astype(BF16)
    q_arrive()
    query_wide[:, 0:HEAD] = query_all[...].reshape(rows, HEAD)

    def scores(c):
        part = pl.ds(pl.multiple_of(c * block, block), block)
        slot = lax.broadcasted_iota(jnp.int32, (block, LANES), 0)
        beyond = jnp.where(slot >= visible[0:1, :] - c * block, 1.0, 0.0).astype(BF16)
        return dot_across(
            jnp.concatenate([key_buf[part, :], beyond], axis=1), query_wide[...]
        )

    def absorb(c, slot):
        part = pl.ds(pl.multiple_of(c * block, block), block)
        s = score_buf[slot]
        old = high[0:1, :]
        new = jnp.maximum(old, jnp.max(s, axis=0, keepdims=True))
        weights = jnp.exp2((s - new) * base).astype(BF16)
        rescale = jnp.exp2((old - new) * base)
        high[...] = jnp.broadcast_to(new, high.shape)
        upright = jnp.concatenate(
            [value_buf[part, :].T, jnp.ones((16, block), BF16)], axis=0
        )
        update = dot(upright, weights)
        acc[...] = acc[...] * rescale + update[0:HEAD]
        total[...] = total[...] * rescale + update[HEAD : HEAD + 8]

    key_copy(0).wait()
    score_buf[0] = scores(0)

    def visit(i, _):
        c = 2 * i
        key_copy(c + 1).wait()
        value_copy(c).wait()
        key_copy(c + 2).wait()
        value_copy(c + 1).wait()
        score_buf[1] = scores(c + 1)
        absorb(c, 0)
        score_buf[0] = scores(c + 2)
        absorb(c + 1, 1)
        return 0

    lax.fori_loop(0, turns // 2 - 1, visit, 0)
    key_copy(turns - 1).wait()
    value_copy(turns - 2).wait()
    value_copy(turns - 1).wait()
    score_buf[1] = scores(turns - 1)
    absorb(turns - 2, 0)
    absorb(turns - 1, 1)

    high_row = high[0:1, :]
    total_row = total[0:1, :]
    part_send[:, 0:32, :] = (
        (acc[...] / total_row).T.astype(BF16).reshape(ctxs, 32, HEAD)
    )

    def piece(v):
        return v.astype(BF16).astype(F32)

    h1 = piece(high_row)
    h2 = piece(high_row - h1)
    h3 = piece(high_row - h1 - h2)
    t1 = piece(total_row)
    t2 = piece(total_row - t1)
    index = lax.broadcasted_iota(jnp.int32, (16, rows), 0)
    stats = jnp.zeros((16, rows), F32)
    for k, v in enumerate((h1, h2, h3, t1, t2)):
        stats = jnp.where(index == k, v, stats)
    stats = stats.astype(BF16)
    for i in range(ctxs):
        at = i // 4 * LANES
        part_send[i, 32:48, :] = stats[:, at : at + LANES]
    part_recv[ctx] = part_send[ctx]
    p_start, p_arrive, p_sent = over_ctx(1, lambda other: part_send.at[other], part_recv)
    p_start()
    q_sent()
    p_arrive()

    tops = []
    sums = []
    for i in range(ctxs):
        tile = part_recv[i, 32:48, :].astype(F32)
        tops.append(tile[0:1] + tile[1:2] + tile[2:3])
        sums.append(tile[3:4] + tile[4:5])
    tops = jnp.concatenate(tops, axis=0)
    sums = jnp.concatenate(sums, axis=0)
    shares = sums * jnp.exp2((tops - jnp.max(tops, axis=0, keepdims=True)) * base)
    shares = shares / jnp.sum(shares, axis=0, keepdims=True)
    square_tile[...] = jnp.zeros(square_tile.shape, F32)
    square_tile[0:ctxs, :] = shares
    square_tile[...] = square_tile[...].T
    mine = square_tile[pl.ds(pl.multiple_of(lax.rem(ctx, 4) * 32, 32), 32), :]
    merged = jnp.zeros((32, HEAD), F32)
    for i in range(ctxs):
        merged = merged + part_recv[i, 0:32, :].astype(F32) * mine[:, i : i + 1]
    rows_send[...] = merged.astype(BF16)
    rows_all[ctx] = rows_send[...]
    r_start, r_arrive, r_sent = over_ctx(2, lambda other: rows_send, rows_all)
    r_start()
    rows_f32[...] = rows_send[...].astype(F32)
    for g in range(GROUPS):
        attended[:, g * HEAD : (g + 1) * HEAD] = rows_f32[pl.ds(g, 4, stride=GROUPS), :].astype(
            BF16
        )
    p_sent()
    weight_copies[0].wait()
    r_arrive()

    wide_f32[...] = rows_all[...].astype(F32).reshape(rows, HEAD)
    projected = jnp.zeros((batch, width), F32)
    for g in range(GROUPS):
        lines = wide_f32[pl.ds(g, batch, stride=GROUPS), :].astype(BF16)
        projected = projected + dot_across(lines, wo_buf[:, g * HEAD : (g + 1) * HEAD])
    proj_all[head] = projected.astype(BF16)
    d_start, d_arrive, d_sent = over_head(0, lambda other: proj_all.at[head], proj_all)
    d_start()
    r_sent()
    d_arrive()

    combined = residual[...].astype(F32)
    mixed = proj_all[0].astype(F32)
    for i in range(1, heads):
        mixed = mixed + proj_all[i].astype(F32)
    combined = combined + mixed
    stream[...] = combined.astype(BF16)
    squares = jnp.sum(combined * combined, axis=1, keepdims=True)
    normed = (combined * gain[...]).astype(BF16)

    tall = 16 * ctxs
    spread = jnp.where(
        lax.broadcasted_iota(jnp.int32, (tall, batch), 0) // 16 * 4
        + lax.broadcasted_iota(jnp.int32, (tall, batch), 0) % 4
        == lax.broadcasted_iota(jnp.int32, (tall, batch), 1),
        1.0,
        0.0,
    ).astype(BF16)
    copies = dot(spread, normed)
    which = lax.broadcasted_iota(jnp.int32, (tall, width), 0) % 16 // 4
    for k in range(4):
        lhs[:, k * width : (k + 1) * width] = jnp.where(which == k, copies, 0.0).astype(BF16)
    s1 = squares.astype(BF16).astype(F32)
    s2 = squares - s1
    lane = lax.broadcasted_iota(jnp.int32, (batch, LANES), 1)
    marks = jnp.where(lane == 0, s1, jnp.where(lane == 1, s2, 0.0)).astype(BF16)
    gate_send[:, :, first : first + LANES] = (
        dot(spread, marks).astype(BF16).reshape(ctxs, 16, LANES)
    )
    for copy in weight_copies[1:5]:
        copy.wait()
    full = lhs[...]
    for at in range(0, second, 256):
        wide = min(256, second - at)
        gate_send[:, :, at : at + wide] = (
            dot(full, pair_buf[:, at : at + wide]).astype(BF16).reshape(ctxs, 16, wide)
        )
    gate_send[:, :, second:first] = (
        dot(full[:, 0 : 2 * width], pair_buf[0 : 2 * width, second:first])
        .astype(BF16)
        .reshape(ctxs, 16, first - second)
    )
    gate_recv[ctx] = gate_send[ctx]
    g_start, g_arrive, g_sent = over_ctx(3, lambda other: gate_send.at[other], gate_recv)
    g_start()
    d_sent()
    g_arrive()

    summed = gate_recv[0].astype(F32)
    for i in range(1, ctxs):
        summed = summed + gate_recv[i].astype(F32)
    square_total = jnp.sum(summed[:, first : first + LANES], axis=1, keepdims=True)
    scaled = summed[:, 0:first] * lax.rsqrt(square_total / model + EPSILON)

    def gated(v):
        return v / (1.0 + jnp.exp(-v)) * pltpu.roll(v, 4, 0)

    upper = gated(scaled[0:8])
    lower = gated(scaled[8:16])
    index = lax.broadcasted_iota(jnp.int32, (8, first), 0)
    hidden_send[...] = jnp.where(index < 4, upper, pltpu.roll(lower, 4, 0)).astype(BF16)
    hidden_all[ctx] = hidden_send[...]
    h_start, h_arrive, h_sent = over_ctx(4, lambda other: hidden_send, hidden_all)
    h_start()
    g_sent()
    weight_copies[5].wait()
    h_arrive()

    hidden = hidden_all[...].astype(F32).reshape(8 * ctxs, first).astype(BF16)
    one = dot_across(hidden, down_buf[:, 0:first])
    two = dot_across(hidden[:, 0:second], down_buf[:, first:hidden_width])
    both = one + pltpu.roll(two, 8 * ctxs - 4, 0)
    index = lax.broadcasted_iota(jnp.int32, (8, width), 0)
    for i in range(heads):
        down_send[i] = jnp.where(
            index < 4,
            both[16 * i : 16 * i + 8],
            pltpu.roll(both[16 * i + 8 : 16 * i + 16], 4, 0),
        )
    down_recv[head] = down_send[head]
    f_start, f_arrive, f_sent = over_head(1, lambda other: down_send.at[other], down_recv)
    f_start()
    h_sent()
    f_arrive()
    result = down_recv[0]
    for i in range(1, heads):
        result = result + down_recv[i]
    ffn_out[...] = result.astype(BF16)
    f_sent()


def local(
    ctxs,
    heads,
    block,
    queries,
    keys,
    values,
    offsets,
    lengths,
    residual,
    wo,
    norm_gain,
    w_gate,
    w_up,
    w_down,
):
    span = keys.shape[0]
    batch, width = residual.shape
    rows = batch * GROUPS
    hidden_width = w_gate.shape[1]
    first = (hidden_width // LANES + 1) // 2 * LANES
    sizes = (ctxs, heads, span, block, width, width * ctxs)
    vmem = pl.BlockSpec(memory_space=pltpu.VMEM)
    smem = pl.BlockSpec(memory_space=pltpu.SMEM)
    hbm = pl.BlockSpec(memory_space=pl.ANY)
    return pl.pallas_call(
        functools.partial(kernel, sizes),
        out_shape=(
            jax.ShapeDtypeStruct(queries.shape, BF16),
            jax.ShapeDtypeStruct((batch, width), BF16),
            jax.ShapeDtypeStruct((batch // heads, width), BF16),
        ),
        in_specs=[vmem, vmem, smem, vmem, vmem] + [hbm] * 6,
        out_specs=(vmem, vmem, vmem),
        scratch_shapes=[
            pltpu.VMEM((span, HEAD), BF16),
            pltpu.VMEM((span, HEAD), BF16),
            pltpu.VMEM((width, rows * HEAD // batch), BF16),
            pltpu.VMEM((4 * width, first), BF16),
            pltpu.VMEM((width, hidden_width), BF16),
            pltpu.VMEM((8, LANES), jnp.int32),
            pltpu.VMEM((32, HEAD), F32),
            pltpu.VMEM((32, HEAD), BF16),
            pltpu.VMEM((ctxs, 32, HEAD), BF16),
            pltpu.VMEM((rows, HEAD + LANES), BF16),
            pltpu.VMEM((2, block, rows), F32),
            pltpu.VMEM((8, rows), F32),
            pltpu.VMEM((8, rows), F32),
            pltpu.VMEM((HEAD, rows), F32),
            pltpu.VMEM((ctxs, 48, HEAD), BF16),
            pltpu.VMEM((ctxs, 48, HEAD), BF16),
            pltpu.VMEM((32, HEAD), F32),
            pltpu.VMEM((32, HEAD), BF16),
            pltpu.VMEM((ctxs, 32, HEAD), BF16),
            pltpu.VMEM((rows, HEAD), F32),
            pltpu.VMEM((heads, batch, width), BF16),
            pltpu.VMEM((LANES, LANES), F32),
            pltpu.VMEM((16 * ctxs, 4 * width), BF16),
            pltpu.VMEM((ctxs, 16, first + LANES), BF16),
            pltpu.VMEM((ctxs, 16, first + LANES), BF16),
            pltpu.VMEM((8, first), BF16),
            pltpu.VMEM((ctxs, 8, first), BF16),
            pltpu.VMEM((heads, 8, width), F32),
            pltpu.VMEM((heads, 8, width), F32),
            pltpu.SemaphoreType.DMA((2, span // block)),
            pltpu.SemaphoreType.DMA((6,)),
            pltpu.SemaphoreType.DMA((5, ctxs)),
            pltpu.SemaphoreType.DMA((5, ctxs)),
            pltpu.SemaphoreType.DMA((2, heads)),
            pltpu.SemaphoreType.DMA((2, heads)),
        ],
        compiler_params=pltpu.CompilerParams(
            collective_id=0, has_side_effects=True, vmem_limit_bytes=60 * 1024 * 1024
        ),
        name="layer",
    )(
        queries,
        lengths.reshape(1, batch),
        offsets,
        residual,
        norm_gain.reshape(1, width),
        keys.reshape(span, HEAD),
        values.reshape(span, HEAD),
        wo.T,
        w_gate,
        w_up,
        w_down.T,
    )


def solution(mesh, block=1024):
    return jax.shard_map(
        functools.partial(local, mesh.shape["ctx"], mesh.shape["head"], block),
        mesh=mesh,
        in_specs=(
            P("ctx", "head"),
            P("ctx", "head", None),
            P("ctx", "head", None),
            P("ctx"),
            P(),
            P(None, "ctx"),
            P("head", "ctx"),
            P("ctx"),
            P("ctx", "head"),
            P("ctx", "head"),
            P("head", "ctx"),
        ),
        out_specs=(P("ctx", "head"), P(None, "ctx"), P("head", "ctx")),
        check_vma=False,
    )
```

```python
import functools
import math

import jax
import jax.numpy as jnp
from jax import lax
from jax.experimental import pallas as pl
from jax.experimental.pallas import tpu as pltpu
from jax.sharding import PartitionSpec as P

MESH = pl.DeviceIdType.MESH
F32 = jnp.float32
BF16 = jnp.bfloat16
EPSILON = 1e-06
HIDDEN_SCORE = -1e30
GROUPS = 8
HEAD = 128
LANES = 128
EARLY = 16
GRANT = 60 * 1024 * 1024
PIECES = 2


def dot(a, b):
    return jnp.dot(a, b, preferred_element_type=F32)


def dot_across(a, b):
    return lax.dot_general(a, b, (((1,), (1,)), ((), ())), preferred_element_type=F32)


def cuts_of(first):
    step = first // LANES // PIECES // 2 * 2 * LANES
    return [k * step for k in range(PIECES)] + [first]


def kernel(
    sizes,
    offsets,
    queries_in,
    lengths_in,
    residual_in,
    gain_in,
    keys,
    values,
    wo,
    w_gate,
    w_up,
    w_down,
    attended,
    stream,
    ffn_out,
    queries,
    lengths,
    residual,
    gain,
    key_buf,
    value_buf,
    wo_buf,
    pair_buf,
    down_buf,
    visible,
    query_row,
    query_send,
    query_all,
    query_wide,
    score_buf,
    high,
    total,
    acc,
    part_send,
    part_recv,
    rows_f32,
    rows_send,
    rows_all,
    wide_f32,
    proj_all,
    square_tile,
    lhs,
    down_send,
    down_recv,
    load_sem,
    weight_sem,
    small_sem,
    ctx_send,
    ctx_recv,
    head_send,
    head_recv,
    *pieces,
):
    pieces = [pieces[4 * i : 4 * i + 4] for i in range(len(pieces) // 4)]
    cuts = cuts_of(pair_buf.shape[1])
    ctxs, heads, span, block, width, model = sizes
    batch = 4 * ctxs
    rows = batch * GROUPS
    turns = span // block
    hidden_width = w_gate.shape[1]
    first = pair_buf.shape[1]
    second = hidden_width - first
    base = 1.0 / math.sqrt(HEAD) * math.log2(math.e)
    early = min(EARLY, turns)
    ctx = lax.axis_index("ctx")
    head = lax.axis_index("head")

    far = lambda d, n: min(d, n - d)
    sides = (4, 4) if ctxs == 16 else (1, ctxs)
    steps = [(a, b) for a in range(sides[0]) for b in range(sides[1]) if a or b]
    steps.sort(key=lambda t: -far(t[0], sides[0]) - far(t[1], sides[1]))
    major, minor = ctx // sides[1], lax.rem(ctx, sides[1])
    ctx_others = [
        lax.rem(major + a, sides[0]) * sides[1] + lax.rem(minor + b, sides[1]) for a, b in steps
    ]
    chips = heads // 2
    steps = [(a, b) for a in range(chips) for b in range(2) if a or b]
    steps.sort(key=lambda t: -2 * far(t[0], chips) - t[1])
    chip, core = head // 2, lax.rem(head, 2)
    head_others = [lax.rem(chip + a, chips) * 2 + lax.rem(core + b, 2) for a, b in steps]

    def key_copy(c):
        part = pl.ds(pl.multiple_of(c * block, block), block)
        return pltpu.make_async_copy(keys.at[part], key_buf.at[part], load_sem.at[0, c])

    def value_copy(c):
        part = pl.ds(pl.multiple_of(c * block, block), block)
        return pltpu.make_async_copy(values.at[part], value_buf.at[part], load_sem.at[1, c])

    weight_copies = [
        pltpu.make_async_copy(wo, wo_buf, weight_sem.at[0]),
        pltpu.make_async_copy(
            w_gate.at[:, 0:first], pair_buf.at[0:width, :], weight_sem.at[1]
        ),
        pltpu.make_async_copy(
            w_up.at[:, 0:first], pair_buf.at[width : 2 * width, :], weight_sem.at[2]
        ),
        pltpu.make_async_copy(
            w_gate.at[:, first:hidden_width],
            pair_buf.at[2 * width : 3 * width, 0:second],
            weight_sem.at[3],
        ),
        pltpu.make_async_copy(
            w_up.at[:, first:hidden_width],
            pair_buf.at[3 * width : 4 * width, 0:second],
            weight_sem.at[4],
        ),
        pltpu.make_async_copy(w_down, down_buf, weight_sem.at[5]),
    ]

    small_copies = [
        pltpu.make_async_copy(source, target, small_sem.at[i])
        for i, (source, target) in enumerate(
            (
                (queries_in, queries),
                (lengths_in, lengths),
                (residual_in, residual),
                (gain_in, gain),
            )
        )
    ]

    barrier = pltpu.get_barrier_semaphore()
    for other in ctx_others:
        pl.semaphore_signal(barrier, inc=1, device_id={"ctx": other}, device_id_type=MESH)
    for other in head_others:
        pl.semaphore_signal(barrier, inc=1, device_id={"head": other}, device_id_type=MESH)

    def fetch(c, _):
        key_copy(c).start()
        value_copy(c).start()
        return 0

    small_copies[0].start()
    lax.fori_loop(0, early, fetch, 0)

    def exchange(axis, me, others, send_sems, recv_sems, phase, source, slots):
        def one(other, mine):
            return pltpu.make_async_remote_copy(
                src_ref=source(other),
                dst_ref=slots.at[mine],
                send_sem=send_sems.at[phase, other],
                recv_sem=recv_sems.at[phase, mine],
                device_id={axis: other},
                device_id_type=MESH,
            )

        def start():
            for other in others:
                one(other, me).start()

        def arrive():
            for other in reversed(others):
                one(other, other).wait_recv()

        def sent():
            for other in others:
                one(other, me).wait_send()

        return start, arrive, sent

    over_ctx = functools.partial(exchange, "ctx", ctx, ctx_others, ctx_send, ctx_recv)
    over_head = functools.partial(exchange, "head", head, head_others, head_send, head_recv)

    small_copies[0].wait()
    own = queries[...].astype(F32)
    for g in range(GROUPS):
        query_row[pl.ds(g, 4, stride=GROUPS), :] = own[:, g * HEAD : (g + 1) * HEAD]
    query_send[...] = query_row[...].astype(BF16)
    query_all[ctx] = query_send[...]

    pl.semaphore_wait(barrier, ctxs - 1 + heads - 1)
    q_start, q_arrive, q_sent = over_ctx(0, lambda other: query_send, query_all)
    q_start()
    for copy in small_copies[1:]:
        copy.start()
    lax.fori_loop(early, turns, fetch, 0)
    for copy in weight_copies:
        copy.start()
    for copy in small_copies[1:]:
        copy.wait()

    visible[...] = jnp.full(visible.shape, 2**30, jnp.int32)
    visible[0:1, 0:batch] = lengths[...] - offsets[0]
    high[...] = jnp.full(high.shape, -3e38, F32)
    total[...] = jnp.zeros(total.shape, F32)
    acc[...] = jnp.zeros(acc.shape, F32)
    row_of = lax.broadcasted_iota(jnp.int32, (rows, LANES), 0) // GROUPS
    column = lax.broadcasted_iota(jnp.int32, (rows, LANES), 1)
    query_wide[:, HEAD : HEAD + LANES] = jnp.where(row_of == column, HIDDEN_SCORE, 0.0).astype(BF16)
    q_arrive()
    query_wide[:, 0:HEAD] = query_all[...].reshape(rows, HEAD)

    def scores(c):
        part = pl.ds(pl.multiple_of(c * block, block), block)
        slot = lax.broadcasted_iota(jnp.int32, (block, LANES), 0)
        beyond = jnp.where(slot >= visible[0:1, :] - c * block, 1.0, 0.0).astype(BF16)
        return dot_across(
            jnp.concatenate([key_buf[part, :], beyond], axis=1), query_wide[...]
        )

    def absorb(c, slot):
        part = pl.ds(pl.multiple_of(c * block, block), block)
        s = score_buf[slot]
        old = high[0:1, :]
        new = jnp.maximum(old, jnp.max(s, axis=0, keepdims=True))
        weights = jnp.exp2((s - new) * base).astype(BF16)
        rescale = jnp.exp2((old - new) * base)
        high[...] = jnp.broadcast_to(new, high.shape)
        upright = jnp.concatenate(
            [value_buf[part, :].T, jnp.ones((16, block), BF16)], axis=0
        )
        update = dot(upright, weights)
        acc[...] = acc[...] * rescale + update[0:HEAD]
        total[...] = total[...] * rescale + update[HEAD : HEAD + 8]

    key_copy(0).wait()
    score_buf[0] = scores(0)

    def visit(i, _):
        c = 2 * i
        key_copy(c + 1).wait()
        value_copy(c).wait()
        key_copy(c + 2).wait()
        value_copy(c + 1).wait()
        score_buf[1] = scores(c + 1)
        absorb(c, 0)
        score_buf[0] = scores(c + 2)
        absorb(c + 1, 1)
        return 0

    lax.fori_loop(0, turns // 2 - 1, visit, 0)
    key_copy(turns - 1).wait()
    value_copy(turns - 2).wait()
    value_copy(turns - 1).wait()
    score_buf[1] = scores(turns - 1)
    absorb(turns - 2, 0)
    absorb(turns - 1, 1)

    high_row = high[0:1, :]
    total_row = total[0:1, :]
    part_send[:, 0:32, :] = (
        (acc[...] / total_row).T.astype(BF16).reshape(ctxs, 32, HEAD)
    )

    def piece(v):
        return v.astype(BF16).astype(F32)

    h1 = piece(high_row)
    h2 = piece(high_row - h1)
    h3 = piece(high_row - h1 - h2)
    t1 = piece(total_row)
    t2 = piece(total_row - t1)
    index = lax.broadcasted_iota(jnp.int32, (16, rows), 0)
    stats = jnp.zeros((16, rows), F32)
    for k, v in enumerate((h1, h2, h3, t1, t2)):
        stats = jnp.where(index == k, v, stats)
    stats = stats.astype(BF16)
    for i in range(ctxs):
        at = i // 4 * LANES
        part_send[i, 32:48, :] = stats[:, at : at + LANES]
    part_recv[ctx] = part_send[ctx]
    p_start, p_arrive, p_sent = over_ctx(1, lambda other: part_send.at[other], part_recv)
    p_start()
    q_sent()
    p_arrive()

    tops = []
    sums = []
    for i in range(ctxs):
        tile = part_recv[i, 32:48, :].astype(F32)
        tops.append(tile[0:1] + tile[1:2] + tile[2:3])
        sums.append(tile[3:4] + tile[4:5])
    tops = jnp.concatenate(tops, axis=0)
    sums = jnp.concatenate(sums, axis=0)
    shares = sums * jnp.exp2((tops - jnp.max(tops, axis=0, keepdims=True)) * base)
    shares = shares / jnp.sum(shares, axis=0, keepdims=True)
    square_tile[...] = jnp.zeros(square_tile.shape, F32)
    square_tile[0:ctxs, :] = shares
    square_tile[...] = square_tile[...].T
    mine = square_tile[pl.ds(pl.multiple_of(lax.rem(ctx, 4) * 32, 32), 32), :]
    merged = jnp.zeros((32, HEAD), F32)
    for i in range(ctxs):
        merged = merged + part_recv[i, 0:32, :].astype(F32) * mine[:, i : i + 1]
    rows_send[...] = merged.astype(BF16)
    rows_all[ctx] = rows_send[...]
    r_start, r_arrive, r_sent = over_ctx(2, lambda other: rows_send, rows_all)
    r_start()
    rows_f32[...] = rows_send[...].astype(F32)
    for g in range(GROUPS):
        attended[:, g * HEAD : (g + 1) * HEAD] = rows_f32[pl.ds(g, 4, stride=GROUPS), :].astype(
            BF16
        )
    p_sent()
    weight_copies[0].wait()
    r_arrive()

    wide_f32[...] = rows_all[...].astype(F32).reshape(rows, HEAD)
    projected = jnp.zeros((batch, width), F32)
    for g in range(GROUPS):
        lines = wide_f32[pl.ds(g, batch, stride=GROUPS), :].astype(BF16)
        projected = projected + dot_across(lines, wo_buf[:, g * HEAD : (g + 1) * HEAD])
    proj_all[head] = projected.astype(BF16)
    d_start, d_arrive, d_sent = over_head(0, lambda other: proj_all.at[head], proj_all)
    d_start()
    r_sent()
    d_arrive()

    combined = residual[...].astype(F32)
    mixed = proj_all[0].astype(F32)
    for i in range(1, heads):
        mixed = mixed + proj_all[i].astype(F32)
    combined = combined + mixed
    stream[...] = combined.astype(BF16)
    squares = jnp.sum(combined * combined, axis=1, keepdims=True)
    normed = (combined * gain[...].reshape(1, width)).astype(BF16)

    tall = 16 * ctxs
    spread = jnp.where(
        lax.broadcasted_iota(jnp.int32, (tall, batch), 0) // 16 * 4
        + lax.broadcasted_iota(jnp.int32, (tall, batch), 0) % 4
        == lax.broadcasted_iota(jnp.int32, (tall, batch), 1),
        1.0,
        0.0,
    ).astype(BF16)
    copies = dot(spread, normed)
    which = lax.broadcasted_iota(jnp.int32, (tall, width), 0) % 16 // 4
    for k in range(4):
        lhs[:, k * width : (k + 1) * width] = jnp.where(which == k, copies, 0.0).astype(BF16)
    s1 = squares.astype(BF16).astype(F32)
    s2 = squares - s1
    lane = lax.broadcasted_iota(jnp.int32, (batch, LANES), 1)
    marks = jnp.where(lane == 0, s1, jnp.where(lane == 1, s2, 0.0)).astype(BF16)
    pieces[0][0][:, :, cuts[1] : cuts[1] + LANES] = (
        dot(spread, marks).astype(BF16).reshape(ctxs, 16, LANES)
    )
    for copy in weight_copies[1:5]:
        copy.wait()
    full = lhs[...]

    gates = []
    hiddens = []
    for k, (gate_send, gate_recv, hidden_send, hidden_all) in enumerate(pieces):
        low, top = cuts[k : k + 2]
        for at in range(low, min(top, second), 256):
            wide = min(256, min(top, second) - at)
            gate_send[:, :, at - low : at - low + wide] = (
                dot(full, pair_buf[:, at : at + wide]).astype(BF16).reshape(ctxs, 16, wide)
            )
        if top > second:
            gate_send[:, :, second - low : top - low] = (
                dot(full[:, 0 : 2 * width], pair_buf[0 : 2 * width, second:top])
                .astype(BF16)
                .reshape(ctxs, 16, top - second)
            )
        gate_recv[ctx] = gate_send[ctx]
        gates.append(over_ctx(3 + k, lambda other, sent=gate_send: sent.at[other], gate_recv))
        gates[k][0]()
    d_sent()

    def gated(v):
        return v / (1.0 + jnp.exp(-v)) * pltpu.roll(v, 4, 0)

    for k, (gate_send, gate_recv, hidden_send, hidden_all) in enumerate(pieces):
        low, top = cuts[k : k + 2]
        gates[k][1]()
        summed = gate_recv[0].astype(F32)
        for i in range(1, ctxs):
            summed = summed + gate_recv[i].astype(F32)
        if k == 0:
            square_total = jnp.sum(
                summed[:, top : top + LANES], axis=1, keepdims=True
            )
            scale = lax.rsqrt(square_total / model + EPSILON)
        scaled = summed[:, 0 : top - low] * scale
        upper = gated(scaled[0:8])
        lower = gated(scaled[8:16])
        index = lax.broadcasted_iota(jnp.int32, upper.shape, 0)
        hidden_send[...] = jnp.where(index < 4, upper, pltpu.roll(lower, 4, 0)).astype(BF16)
        hidden_all[ctx] = hidden_send[...]
        hiddens.append(
            over_ctx(3 + len(pieces) + k, lambda other, sent=hidden_send: sent, hidden_all)
        )
        hiddens[k][0]()
    weight_copies[5].wait()
    one = jnp.zeros((8 * ctxs, width), F32)
    two = jnp.zeros((8 * ctxs, width), F32)
    for k, (gate_send, gate_recv, hidden_send, hidden_all) in enumerate(pieces):
        low, top = cuts[k : k + 2]
        hiddens[k][1]()
        hidden = hidden_all[...].astype(F32).reshape(8 * ctxs, top - low).astype(BF16)
        one = one + dot_across(hidden, down_buf[:, low:top])
        rest = min(top, second) - low
        two = two + dot_across(hidden[:, 0:rest], down_buf[:, first + low : first + low + rest])
    both = one + pltpu.roll(two, 8 * ctxs - 4, 0)
    index = lax.broadcasted_iota(jnp.int32, (8, width), 0)
    for i in range(heads):
        down_send[i] = jnp.where(
            index < 4,
            both[16 * i : 16 * i + 8],
            pltpu.roll(both[16 * i + 8 : 16 * i + 16], 4, 0),
        ).astype(BF16)
    down_recv[head] = down_send[head]
    f_start, f_arrive, f_sent = over_head(1, lambda other: down_send.at[other], down_recv)
    f_start()
    for k in range(len(pieces)):
        gates[k][2]()
        hiddens[k][2]()
    f_arrive()
    result = down_recv[0].astype(F32)
    for i in range(1, heads):
        result = result + down_recv[i].astype(F32)
    ffn_out[...] = result.astype(BF16)
    f_sent()


def hand_over(a_in, b_in, c_in, a, b, c, sem):
    copies = [
        pltpu.make_async_copy(source, target, sem.at[i])
        for i, (source, target) in enumerate(((a_in, a), (b_in, b), (c_in, c)))
    ]
    for copy in copies:
        copy.start()
    for copy in copies:
        copy.wait()


def local(
    ctxs,
    heads,
    block,
    queries,
    keys,
    values,
    offsets,
    lengths,
    residual,
    wo,
    norm_gain,
    w_gate,
    w_up,
    w_down,
):
    span = keys.shape[0]
    batch, width = residual.shape
    rows = batch * GROUPS
    hidden_width = w_gate.shape[1]
    first = (hidden_width // LANES + 1) // 2 * LANES
    cuts = cuts_of(first)
    slabs = []
    for k in range(PIECES):
        wide = cuts[k + 1] - cuts[k]
        more = 0 if k else LANES
        slabs += [
            pltpu.VMEM((ctxs, 16, wide + more), BF16),
            pltpu.VMEM((ctxs, 16, wide + more), BF16),
            pltpu.VMEM((8, wide), BF16),
            pltpu.VMEM((ctxs, 8, wide), BF16),
        ]
    sizes = (ctxs, heads, span, block, width, width * ctxs)
    vmem = pl.BlockSpec(memory_space=pltpu.VMEM)
    hbm = pl.BlockSpec(memory_space=pltpu.HBM)
    smem = pl.BlockSpec(memory_space=pltpu.SMEM)
    free = pl.BlockSpec(memory_space=pl.ANY)
    outs = (
        jax.ShapeDtypeStruct(queries.shape, BF16),
        jax.ShapeDtypeStruct((batch, width), BF16),
        jax.ShapeDtypeStruct((batch // heads, width), BF16),
    )
    results = pl.pallas_call(
        functools.partial(kernel, sizes),
        out_shape=tuple(pltpu.VMEM(o.shape, o.dtype) for o in outs),
        in_specs=[smem] + [hbm] * 10,
        out_specs=(vmem, vmem, vmem),
        scratch_shapes=[
            pltpu.VMEM(queries.shape, BF16),
            pltpu.VMEM((1, batch), jnp.int32),
            pltpu.VMEM(residual.shape, BF16),
            pltpu.VMEM((width,), F32),
            pltpu.VMEM((span, HEAD), BF16),
            pltpu.VMEM((span, HEAD), BF16),
            pltpu.VMEM((width, rows * HEAD // batch), BF16),
            pltpu.VMEM((4 * width, first), BF16),
            pltpu.VMEM((width, hidden_width), BF16),
            pltpu.VMEM((8, LANES), jnp.int32),
            pltpu.VMEM((32, HEAD), F32),
            pltpu.VMEM((32, HEAD), BF16),
            pltpu.VMEM((ctxs, 32, HEAD), BF16),
            pltpu.VMEM((rows, HEAD + LANES), BF16),
            pltpu.VMEM((2, block, rows), F32),
            pltpu.VMEM((8, rows), F32),
            pltpu.VMEM((8, rows), F32),
            pltpu.VMEM((HEAD, rows), F32),
            pltpu.VMEM((ctxs, 48, HEAD), BF16),
            pltpu.VMEM((ctxs, 48, HEAD), BF16),
            pltpu.VMEM((32, HEAD), F32),
            pltpu.VMEM((32, HEAD), BF16),
            pltpu.VMEM((ctxs, 32, HEAD), BF16),
            pltpu.VMEM((rows, HEAD), F32),
            pltpu.VMEM((heads, batch, width), BF16),
            pltpu.VMEM((LANES, LANES), F32),
            pltpu.VMEM((16 * ctxs, 4 * width), BF16),
            pltpu.VMEM((heads, 8, width), BF16),
            pltpu.VMEM((heads, 8, width), BF16),
            pltpu.SemaphoreType.DMA((2, span // block)),
            pltpu.SemaphoreType.DMA((6,)),
            pltpu.SemaphoreType.DMA((4,)),
            pltpu.SemaphoreType.DMA((3 + 2 * PIECES, ctxs)),
            pltpu.SemaphoreType.DMA((3 + 2 * PIECES, ctxs)),
            pltpu.SemaphoreType.DMA((2, heads)),
            pltpu.SemaphoreType.DMA((2, heads)),
        ]
        + slabs,
        compiler_params=pltpu.CompilerParams(
            collective_id=0, has_side_effects=True, vmem_limit_bytes=GRANT
        ),
        name="layer",
    )(
        offsets,
        *(
            pltpu.with_memory_space_constraint(x, pltpu.HBM)
            for x in (
                queries,
                lengths.reshape(1, batch),
                residual,
                norm_gain,
                keys.reshape(span, HEAD),
                values.reshape(span, HEAD),
                wo.T,
                w_gate,
                w_up,
                w_down.T,
            )
        )
    )
    return pl.pallas_call(
        hand_over,
        out_shape=outs,
        in_specs=[free] * 3,
        out_specs=(free,) * 3,
        scratch_shapes=[pltpu.SemaphoreType.DMA((3,))],
        compiler_params=pltpu.CompilerParams(vmem_limit_bytes=1024 * 1024),
        name="hand_over",
    )(*results)


def solution(mesh, block=2048):
    return jax.shard_map(
        functools.partial(local, mesh.shape["ctx"], mesh.shape["head"], block),
        mesh=mesh,
        in_specs=(
            P("ctx", "head"),
            P("ctx", "head", None),
            P("ctx", "head", None),
            P("ctx"),
            P(),
            P(None, "ctx"),
            P("head", "ctx"),
            P("ctx"),
            P("ctx", "head"),
            P("ctx", "head"),
            P("head", "ctx"),
        ),
        out_specs=(P("ctx", "head"), P(None, "ctx"), P("head", "ctx")),
        check_vma=False,
    )
```

```python
import functools
import math

import jax
import jax.numpy as jnp
from jax import lax
from jax.experimental import pallas as pl
from jax.experimental.pallas import tpu as pltpu
from jax.sharding import PartitionSpec as P

MESH = pl.DeviceIdType.MESH
F32 = jnp.float32
BF16 = jnp.bfloat16
EPSILON = 1e-06
HIDDEN_SCORE = -1e30
GROUPS = 8
HEAD = 128
LANES = 128
EARLY = 16
GRANT = 60 * 1024 * 1024
PIECES = 2


def dot(a, b):
    return jnp.dot(a, b, preferred_element_type=F32)


def dot_across(a, b):
    return lax.dot_general(a, b, (((1,), (1,)), ((), ())), preferred_element_type=F32)


def cuts_of(first):
    step = first // LANES // PIECES // 2 * 2 * LANES
    edges = [k * step for k in range(PIECES)] + [first]
    return [(edges[k], edges[k + 1]) for k in reversed(range(PIECES))]


def kernel(
    sizes,
    offsets,
    queries_in,
    lengths_in,
    residual_in,
    gain_in,
    keys,
    values,
    wo,
    w_gate,
    w_up,
    w_down,
    attended,
    stream,
    ffn_out,
    queries,
    lengths,
    residual,
    gain,
    key_buf,
    value_buf,
    wo_buf,
    pair_buf,
    down_buf,
    visible,
    query_row,
    query_send,
    query_all,
    query_wide,
    score_buf,
    high,
    total,
    acc,
    part_send,
    part_recv,
    rows_f32,
    rows_send,
    rows_all,
    wide_f32,
    proj_all,
    square_tile,
    lhs,
    down_send,
    down_recv,
    load_sem,
    weight_sem,
    small_sem,
    ctx_send,
    ctx_recv,
    head_send,
    head_recv,
    *pieces,
):
    pieces = [pieces[4 * i : 4 * i + 4] for i in range(len(pieces) // 4)]
    cuts = cuts_of(pair_buf.shape[1])
    ctxs, heads, span, block, width, model = sizes
    batch = 4 * ctxs
    rows = batch * GROUPS
    turns = span // block
    hidden_width = w_gate.shape[1]
    first = pair_buf.shape[1]
    second = hidden_width - first
    base = 1.0 / math.sqrt(HEAD) * math.log2(math.e)
    early = min(EARLY, turns)
    ctx = lax.axis_index("ctx")
    head = lax.axis_index("head")

    far = lambda d, n: min(d, n - d)
    sides = (4, 4) if ctxs == 16 else (1, ctxs)
    steps = [(a, b) for a in range(sides[0]) for b in range(sides[1]) if a or b]
    steps.sort(key=lambda t: -far(t[0], sides[0]) - far(t[1], sides[1]))
    major, minor = ctx // sides[1], lax.rem(ctx, sides[1])
    ctx_others = [
        lax.rem(major + a, sides[0]) * sides[1] + lax.rem(minor + b, sides[1]) for a, b in steps
    ]
    chips = heads // 2
    steps = [(a, b) for a in range(chips) for b in range(2) if a or b]
    steps.sort(key=lambda t: -2 * far(t[0], chips) - t[1])
    chip, core = head // 2, lax.rem(head, 2)
    head_others = [lax.rem(chip + a, chips) * 2 + lax.rem(core + b, 2) for a, b in steps]

    def key_copy(c):
        part = pl.ds(pl.multiple_of(c * block, block), block)
        return pltpu.make_async_copy(keys.at[part], key_buf.at[part], load_sem.at[0, c])

    def value_copy(c):
        part = pl.ds(pl.multiple_of(c * block, block), block)
        return pltpu.make_async_copy(values.at[part], value_buf.at[part], load_sem.at[1, c])

    weight_copies = [
        pltpu.make_async_copy(wo, wo_buf, weight_sem.at[0]),
        pltpu.make_async_copy(
            w_gate.at[:, 0:first], pair_buf.at[0:width, :], weight_sem.at[1]
        ),
        pltpu.make_async_copy(
            w_up.at[:, 0:first], pair_buf.at[width : 2 * width, :], weight_sem.at[2]
        ),
        pltpu.make_async_copy(
            w_gate.at[:, first:hidden_width],
            pair_buf.at[2 * width : 3 * width, 0:second],
            weight_sem.at[3],
        ),
        pltpu.make_async_copy(
            w_up.at[:, first:hidden_width],
            pair_buf.at[3 * width : 4 * width, 0:second],
            weight_sem.at[4],
        ),
        pltpu.make_async_copy(w_down, down_buf, weight_sem.at[5]),
    ]

    small_copies = [
        pltpu.make_async_copy(source, target, small_sem.at[i])
        for i, (source, target) in enumerate(
            (
                (queries_in, queries),
                (lengths_in, lengths),
                (residual_in, residual),
                (gain_in, gain),
            )
        )
    ]

    barrier = pltpu.get_barrier_semaphore()
    for other in ctx_others:
        pl.semaphore_signal(barrier, inc=1, device_id={"ctx": other}, device_id_type=MESH)
    for other in head_others:
        pl.semaphore_signal(barrier, inc=1, device_id={"head": other}, device_id_type=MESH)

    def fetch(c, _):
        key_copy(c).start()
        value_copy(c).start()
        return 0

    small_copies[0].start()
    lax.fori_loop(0, early, fetch, 0)

    def exchange(axis, me, others, send_sems, recv_sems, phase, source, slots):
        def one(other, mine):
            return pltpu.make_async_remote_copy(
                src_ref=source(other),
                dst_ref=slots.at[mine],
                send_sem=send_sems.at[phase, other],
                recv_sem=recv_sems.at[phase, mine],
                device_id={axis: other},
                device_id_type=MESH,
            )

        def start():
            for other in others:
                one(other, me).start()

        def arrive():
            for other in reversed(others):
                one(other, other).wait_recv()

        def sent():
            for other in others:
                one(other, me).wait_send()

        return start, arrive, sent

    over_ctx = functools.partial(exchange, "ctx", ctx, ctx_others, ctx_send, ctx_recv)
    over_head = functools.partial(exchange, "head", head, head_others, head_send, head_recv)

    small_copies[0].wait()
    own = queries[...].astype(F32)
    for g in range(GROUPS):
        query_row[pl.ds(g, 4, stride=GROUPS), :] = own[:, g * HEAD : (g + 1) * HEAD]
    query_send[...] = query_row[...].astype(BF16)
    query_all[ctx] = query_send[...]

    pl.semaphore_wait(barrier, ctxs - 1 + heads - 1)
    q_start, q_arrive, q_sent = over_ctx(0, lambda other: query_send, query_all)
    q_start()
    for copy in small_copies[1:]:
        copy.start()
    lax.fori_loop(early, turns, fetch, 0)
    for copy in weight_copies:
        copy.start()
    for copy in small_copies[1:]:
        copy.wait()

    visible[...] = jnp.full(visible.shape, 2**30, jnp.int32)
    visible[0:1, 0:batch] = lengths[...] - offsets[0]
    high[...] = jnp.full(high.shape, -3e38, F32)
    total[...] = jnp.zeros(total.shape, F32)
    acc[...] = jnp.zeros(acc.shape, F32)
    row_of = lax.broadcasted_iota(jnp.int32, (rows, LANES), 0) // GROUPS
    column = lax.broadcasted_iota(jnp.int32, (rows, LANES), 1)
    query_wide[:, HEAD : HEAD + LANES] = jnp.where(row_of == column, HIDDEN_SCORE, 0.0).astype(BF16)
    q_arrive()
    query_wide[:, 0:HEAD] = query_all[...].reshape(rows, HEAD)

    def scores(c):
        part = pl.ds(pl.multiple_of(c * block, block), block)
        slot = lax.broadcasted_iota(jnp.int32, (block, LANES), 0)
        beyond = jnp.where(slot >= visible[0:1, :] - c * block, 1.0, 0.0).astype(BF16)
        return dot_across(
            jnp.concatenate([key_buf[part, :], beyond], axis=1), query_wide[...]
        )

    def absorb(c, slot):
        part = pl.ds(pl.multiple_of(c * block, block), block)
        s = score_buf[slot]
        old = high[0:1, :]
        new = jnp.maximum(old, jnp.max(s, axis=0, keepdims=True))
        weights = jnp.exp2((s - new) * base).astype(BF16)
        rescale = jnp.exp2((old - new) * base)
        high[...] = jnp.broadcast_to(new, high.shape)
        upright = jnp.concatenate(
            [value_buf[part, :].T, jnp.ones((16, block), BF16)], axis=0
        )
        update = dot(upright, weights)
        acc[...] = acc[...] * rescale + update[0:HEAD]
        total[...] = total[...] * rescale + update[HEAD : HEAD + 8]

    key_copy(0).wait()
    score_buf[0] = scores(0)

    def visit(i, _):
        c = 2 * i
        key_copy(c + 1).wait()
        value_copy(c).wait()
        key_copy(c + 2).wait()
        value_copy(c + 1).wait()
        score_buf[1] = scores(c + 1)
        absorb(c, 0)
        score_buf[0] = scores(c + 2)
        absorb(c + 1, 1)
        return 0

    lax.fori_loop(0, turns // 2 - 1, visit, 0)
    key_copy(turns - 1).wait()
    value_copy(turns - 2).wait()
    value_copy(turns - 1).wait()
    score_buf[1] = scores(turns - 1)
    absorb(turns - 2, 0)
    absorb(turns - 1, 1)

    high_row = high[0:1, :]
    total_row = total[0:1, :]
    part_send[:, 0:32, :] = (
        (acc[...] / total_row).astype(BF16).T.reshape(ctxs, 32, HEAD)
    )

    def piece(v):
        return v.astype(BF16).astype(F32)

    h1 = piece(high_row)
    h2 = piece(high_row - h1)
    h3 = piece(high_row - h1 - h2)
    t1 = piece(total_row)
    t2 = piece(total_row - t1)
    index = lax.broadcasted_iota(jnp.int32, (16, rows), 0)
    stats = jnp.zeros((16, rows), F32)
    for k, v in enumerate((h1, h2, h3, t1, t2)):
        stats = jnp.where(index == k, v, stats)
    stats = stats.astype(BF16)
    for i in range(ctxs):
        at = i // 4 * LANES
        part_send[i, 32:48, :] = stats[:, at : at + LANES]
    part_recv[ctx] = part_send[ctx]
    p_start, p_arrive, p_sent = over_ctx(1, lambda other: part_send.at[other], part_recv)
    p_start()
    q_sent()
    p_arrive()

    tops = []
    sums = []
    for i in range(ctxs):
        tile = part_recv[i, 32:48, :].astype(F32)
        tops.append(tile[0:1] + tile[1:2] + tile[2:3])
        sums.append(tile[3:4] + tile[4:5])
    tops = jnp.concatenate(tops, axis=0)
    sums = jnp.concatenate(sums, axis=0)
    shares = sums * jnp.exp2((tops - jnp.max(tops, axis=0, keepdims=True)) * base)
    shares = shares / jnp.sum(shares, axis=0, keepdims=True)
    square_tile[...] = jnp.zeros(square_tile.shape, F32)
    square_tile[0:ctxs, :] = shares
    square_tile[...] = square_tile[...].T
    mine = square_tile[pl.ds(pl.multiple_of(lax.rem(ctx, 4) * 32, 32), 32), :]
    merged = jnp.zeros((32, HEAD), F32)
    for i in range(ctxs):
        merged = merged + part_recv[i, 0:32, :].astype(F32) * mine[:, i : i + 1]
    rows_send[...] = merged.astype(BF16)
    rows_all[ctx] = rows_send[...]
    r_start, r_arrive, r_sent = over_ctx(2, lambda other: rows_send, rows_all)
    r_start()
    rows_f32[...] = rows_send[...].astype(F32)
    for g in range(GROUPS):
        attended[:, g * HEAD : (g + 1) * HEAD] = rows_f32[pl.ds(g, 4, stride=GROUPS), :].astype(
            BF16
        )
    p_sent()
    weight_copies[0].wait()
    r_arrive()

    kept = width - 64
    quarter = batch // 4

    def pack(v):
        parts = [v[i * quarter : (i + 1) * quarter, kept:width] for i in range(4)]
        return jnp.concatenate([v[:, 0:kept], jnp.concatenate(parts, axis=1)], axis=0)

    def unpack(v):
        parts = [v[batch : batch + quarter, i * 64 : (i + 1) * 64] for i in range(4)]
        return jnp.concatenate([v[0:batch], jnp.concatenate(parts, axis=0)], axis=1)

    wide_f32[...] = rows_all[...].astype(F32).reshape(rows, HEAD)
    projected = jnp.zeros((batch, width), F32)
    for g in range(GROUPS):
        lines = wide_f32[pl.ds(g, batch, stride=GROUPS), :].astype(BF16)
        projected = projected + dot_across(lines, wo_buf[:, g * HEAD : (g + 1) * HEAD])
    proj_all[head] = pack(projected).astype(BF16)
    d_start, d_arrive, d_sent = over_head(0, lambda other: proj_all.at[head], proj_all)
    d_start()
    r_sent()
    d_arrive()

    mixed = proj_all[0].astype(F32)
    for i in range(1, heads):
        mixed = mixed + proj_all[i].astype(F32)
    combined = residual[...].astype(F32) + unpack(mixed)
    stream[...] = combined.astype(BF16)
    squares = jnp.sum(combined * combined, axis=1, keepdims=True)
    normed = (combined * gain[...].reshape(1, width)).astype(BF16)

    tall = 16 * ctxs
    spread = jnp.where(
        lax.broadcasted_iota(jnp.int32, (tall, batch), 0) // 16 * 4
        + lax.broadcasted_iota(jnp.int32, (tall, batch), 0) % 4
        == lax.broadcasted_iota(jnp.int32, (tall, batch), 1),
        1.0,
        0.0,
    ).astype(BF16)
    copies = dot(spread, normed)
    which = lax.broadcasted_iota(jnp.int32, (tall, width), 0) % 16 // 4
    for k in range(4):
        lhs[:, k * width : (k + 1) * width] = jnp.where(which == k, copies, 0.0).astype(BF16)
    s1 = squares.astype(BF16).astype(F32)
    s2 = squares - s1
    lane = lax.broadcasted_iota(jnp.int32, (batch, LANES), 1)
    marks = jnp.where(lane == 0, s1, jnp.where(lane == 1, s2, 0.0)).astype(BF16)
    marks = dot(spread, marks)
    for copy in weight_copies[1:5]:
        copy.wait()
    full = lhs[...]

    gates = []
    hiddens = []
    for k, (gate_send, gate_recv, hidden_send, hidden_all) in enumerate(pieces):
        low, top = cuts[k]
        for at in range(low, min(top, second), 256):
            wide = min(256, min(top, second) - at)
            gate_send[:, :, at - low : at - low + wide] = (
                dot(full, pair_buf[:, at : at + wide]).astype(BF16).reshape(ctxs, 16, wide)
            )
        if top > second:
            gate_send[:, :, second - low : top - low] = (
                jnp.where(
                    lax.broadcasted_iota(jnp.int32, (tall, LANES), 0) % 16 < 8,
                    dot(full[:, 0 : 2 * width], pair_buf[0 : 2 * width, second:top]),
                    marks,
                )
                .astype(BF16)
                .reshape(ctxs, 16, top - second)
            )
        gate_recv[ctx] = gate_send[ctx]
        gates.append(over_ctx(3 + k, lambda other, sent=gate_send: sent.at[other], gate_recv))
        gates[k][0]()
    d_sent()

    def gated(v):
        return v / (1.0 + jnp.exp(-v)) * pltpu.roll(v, 4, 0)

    for k, (gate_send, gate_recv, hidden_send, hidden_all) in enumerate(pieces):
        low, top = cuts[k]
        gates[k][1]()
        summed = gate_recv[0].astype(F32)
        for i in range(1, ctxs):
            summed = summed + gate_recv[i].astype(F32)
        if k == 0:
            square_total = jnp.sum(summed[8:16, second - low : top - low], axis=1, keepdims=True)
            scale = lax.rsqrt(square_total / model + EPSILON)
            scale = jnp.concatenate([scale, scale], axis=0)
        scaled = summed[:, 0 : top - low] * scale
        upper = gated(scaled[0:8])
        lower = gated(scaled[8:16])
        index = lax.broadcasted_iota(jnp.int32, upper.shape, 0)
        hidden_send[...] = jnp.where(index < 4, upper, pltpu.roll(lower, 4, 0)).astype(BF16)
        hidden_all[ctx] = hidden_send[...]
        hiddens.append(
            over_ctx(3 + len(pieces) + k, lambda other, sent=hidden_send: sent, hidden_all)
        )
        hiddens[k][0]()
    weight_copies[5].wait()
    one = jnp.zeros((8 * ctxs, width), F32)
    two = jnp.zeros((8 * ctxs, width), F32)
    for k, (gate_send, gate_recv, hidden_send, hidden_all) in enumerate(pieces):
        low, top = cuts[k]
        hiddens[k][1]()
        hidden = hidden_all[...].astype(F32).reshape(8 * ctxs, top - low).astype(BF16)
        one = one + dot_across(hidden, down_buf[:, low:top])
        rest = min(top, second) - low
        two = two + dot_across(hidden[:, 0:rest], down_buf[:, first + low : first + low + rest])
    both = one + pltpu.roll(two, 8 * ctxs - 4, 0)
    index = lax.broadcasted_iota(jnp.int32, (8, width), 0)
    for i in range(heads):
        down_send[i] = jnp.where(
            index < 4,
            both[16 * i : 16 * i + 8],
            pltpu.roll(both[16 * i + 8 : 16 * i + 16], 4, 0),
        ).astype(BF16)
    down_recv[head] = down_send[head]
    f_start, f_arrive, f_sent = over_head(1, lambda other: down_send.at[other], down_recv)
    f_start()
    for k in range(len(pieces)):
        gates[k][2]()
        hiddens[k][2]()
    f_arrive()
    result = down_recv[0].astype(F32)
    for i in range(1, heads):
        result = result + down_recv[i].astype(F32)
    ffn_out[...] = result.astype(BF16)
    f_sent()


def hand_over(a_in, b_in, c_in, a, b, c, sem):
    copies = [
        pltpu.make_async_copy(source, target, sem.at[i])
        for i, (source, target) in enumerate(((a_in, a), (b_in, b), (c_in, c)))
    ]
    for copy in copies:
        copy.start()
    for copy in copies:
        copy.wait()


def local(
    ctxs,
    heads,
    block,
    queries,
    keys,
    values,
    offsets,
    lengths,
    residual,
    wo,
    norm_gain,
    w_gate,
    w_up,
    w_down,
):
    span = keys.shape[0]
    batch, width = residual.shape
    rows = batch * GROUPS
    hidden_width = w_gate.shape[1]
    first = (hidden_width // LANES + 1) // 2 * LANES
    cuts = cuts_of(first)
    slabs = []
    for k in range(PIECES):
        wide = cuts[k][1] - cuts[k][0]
        slabs += [
            pltpu.VMEM((ctxs, 16, wide), BF16),
            pltpu.VMEM((ctxs, 16, wide), BF16),
            pltpu.VMEM((8, wide), BF16),
            pltpu.VMEM((ctxs, 8, wide), BF16),
        ]
    sizes = (ctxs, heads, span, block, width, width * ctxs)
    vmem = pl.BlockSpec(memory_space=pltpu.VMEM)
    hbm = pl.BlockSpec(memory_space=pltpu.HBM)
    smem = pl.BlockSpec(memory_space=pltpu.SMEM)
    free = pl.BlockSpec(memory_space=pl.ANY)
    outs = (
        jax.ShapeDtypeStruct(queries.shape, BF16),
        jax.ShapeDtypeStruct((batch, width), BF16),
        jax.ShapeDtypeStruct((batch // heads, width), BF16),
    )
    results = pl.pallas_call(
        functools.partial(kernel, sizes),
        out_shape=tuple(pltpu.VMEM(o.shape, o.dtype) for o in outs),
        in_specs=[smem] + [hbm] * 10,
        out_specs=(vmem, vmem, vmem),
        scratch_shapes=[
            pltpu.VMEM(queries.shape, BF16),
            pltpu.VMEM((1, batch), jnp.int32),
            pltpu.VMEM(residual.shape, BF16),
            pltpu.VMEM((width,), F32),
            pltpu.VMEM((span, HEAD), BF16),
            pltpu.VMEM((span, HEAD), BF16),
            pltpu.VMEM((width, rows * HEAD // batch), BF16),
            pltpu.VMEM((4 * width, first), BF16),
            pltpu.VMEM((width, hidden_width), BF16),
            pltpu.VMEM((8, LANES), jnp.int32),
            pltpu.VMEM((32, HEAD), F32),
            pltpu.VMEM((32, HEAD), BF16),
            pltpu.VMEM((ctxs, 32, HEAD), BF16),
            pltpu.VMEM((rows, HEAD + LANES), BF16),
            pltpu.VMEM((2, block, rows), F32),
            pltpu.VMEM((8, rows), F32),
            pltpu.VMEM((8, rows), F32),
            pltpu.VMEM((HEAD, rows), F32),
            pltpu.VMEM((ctxs, 48, HEAD), BF16),
            pltpu.VMEM((ctxs, 48, HEAD), BF16),
            pltpu.VMEM((32, HEAD), F32),
            pltpu.VMEM((32, HEAD), BF16),
            pltpu.VMEM((ctxs, 32, HEAD), BF16),
            pltpu.VMEM((rows, HEAD), F32),
            pltpu.VMEM((heads, batch + batch // 4, 256), BF16),
            pltpu.VMEM((LANES, LANES), F32),
            pltpu.VMEM((16 * ctxs, 4 * width), BF16),
            pltpu.VMEM((heads, 8, width), BF16),
            pltpu.VMEM((heads, 8, width), BF16),
            pltpu.SemaphoreType.DMA((2, span // block)),
            pltpu.SemaphoreType.DMA((6,)),
            pltpu.SemaphoreType.DMA((4,)),
            pltpu.SemaphoreType.DMA((3 + 2 * PIECES, ctxs)),
            pltpu.SemaphoreType.DMA((3 + 2 * PIECES, ctxs)),
            pltpu.SemaphoreType.DMA((2, heads)),
            pltpu.SemaphoreType.DMA((2, heads)),
        ]
        + slabs,
        compiler_params=pltpu.CompilerParams(
            collective_id=0, has_side_effects=True, vmem_limit_bytes=GRANT
        ),
        name="layer",
    )(
        offsets,
        *(
            pltpu.with_memory_space_constraint(x, pltpu.HBM)
            for x in (
                queries,
                lengths.reshape(1, batch),
                residual,
                norm_gain,
                keys.reshape(span, HEAD),
                values.reshape(span, HEAD),
                wo.T,
                w_gate,
                w_up,
                w_down.T,
            )
        )
    )
    return pl.pallas_call(
        hand_over,
        out_shape=outs,
        in_specs=[free] * 3,
        out_specs=(free,) * 3,
        scratch_shapes=[pltpu.SemaphoreType.DMA((3,))],
        compiler_params=pltpu.CompilerParams(vmem_limit_bytes=1024 * 1024),
        name="hand_over",
    )(*results)


def solution(mesh, block=4096):
    return jax.shard_map(
        functools.partial(local, mesh.shape["ctx"], mesh.shape["head"], block),
        mesh=mesh,
        in_specs=(
            P("ctx", "head"),
            P("ctx", "head", None),
            P("ctx", "head", None),
            P("ctx"),
            P(),
            P(None, "ctx"),
            P("head", "ctx"),
            P("ctx"),
            P("ctx", "head"),
            P("ctx", "head"),
            P("head", "ctx"),
        ),
        out_specs=(P("ctx", "head"), P(None, "ctx"), P("head", "ctx")),
        check_vma=False,
    )
```

```python
import functools
import math

import jax
import jax.numpy as jnp
from jax import lax
from jax.experimental import pallas as pl
from jax.experimental.pallas import tpu as pltpu
from jax.sharding import PartitionSpec as P

MESH = pl.DeviceIdType.MESH
F32 = jnp.float32
BF16 = jnp.bfloat16
EPSILON = 1e-06
HIDDEN_SCORE = -1e30
GROUPS = 8
HEAD = 128
LANES = 128
EARLY = 16
GRANT = 60 * 1024 * 1024
PIECES = 2


def dot(a, b):
    return jnp.dot(a, b, preferred_element_type=F32)


def dot_across(a, b):
    return lax.dot_general(a, b, (((1,), (1,)), ((), ())), preferred_element_type=F32)


def cuts_of(first):
    step = first // LANES // PIECES // 2 * 2 * LANES
    edges = [k * step for k in range(PIECES)] + [first]
    return [(edges[k], edges[k + 1]) for k in reversed(range(PIECES))]


def kernel(
    sizes,
    offsets,
    queries_in,
    lengths_in,
    residual_in,
    gain_in,
    keys,
    values,
    wo,
    w_gate,
    w_up,
    w_down,
    attended,
    stream,
    ffn_out,
    queries,
    lengths,
    residual,
    gain,
    key_buf,
    value_buf,
    wo_buf,
    pair_buf,
    down_buf,
    visible,
    query_row,
    query_send,
    query_all,
    query_wide,
    score_buf,
    high,
    total,
    acc,
    part_send,
    part_recv,
    rows_f32,
    rows_send,
    rows_all,
    wide_f32,
    proj_all,
    square_tile,
    lhs,
    spread_buf,
    down_send,
    down_recv,
    load_sem,
    weight_sem,
    small_sem,
    ctx_send,
    ctx_recv,
    head_send,
    head_recv,
    *pieces,
):
    pieces = [pieces[4 * i : 4 * i + 4] for i in range(len(pieces) // 4)]
    cuts = cuts_of(pair_buf.shape[1])
    ctxs, heads, span, block, width, model = sizes
    batch = 4 * ctxs
    rows = batch * GROUPS
    turns = span // block
    hidden_width = w_gate.shape[1]
    first = pair_buf.shape[1]
    second = hidden_width - first
    base = 1.0 / math.sqrt(HEAD) * math.log2(math.e)
    early = min(EARLY, turns)
    ctx = lax.axis_index("ctx")
    head = lax.axis_index("head")

    far = lambda d, n: min(d, n - d)
    sides = (4, 4) if ctxs == 16 else (1, ctxs)
    steps = [(a, b) for a in range(sides[0]) for b in range(sides[1]) if a or b]
    steps.sort(key=lambda t: -far(t[0], sides[0]) - far(t[1], sides[1]))
    major, minor = ctx // sides[1], lax.rem(ctx, sides[1])
    ctx_others = [
        lax.rem(major + a, sides[0]) * sides[1] + lax.rem(minor + b, sides[1]) for a, b in steps
    ]
    chips = heads // 2
    steps = [(a, b) for a in range(chips) for b in range(2) if a or b]
    steps.sort(key=lambda t: -2 * far(t[0], chips) - t[1])
    chip, core = head // 2, lax.rem(head, 2)
    head_others = [lax.rem(chip + a, chips) * 2 + lax.rem(core + b, 2) for a, b in steps]

    def key_copy(c):
        part = pl.ds(pl.multiple_of(c * block, block), block)
        return pltpu.make_async_copy(keys.at[part], key_buf.at[part], load_sem.at[0, c])

    def value_copy(c):
        part = pl.ds(pl.multiple_of(c * block, block), block)
        return pltpu.make_async_copy(values.at[part], value_buf.at[part], load_sem.at[1, c])

    weight_copies = [
        pltpu.make_async_copy(wo, wo_buf, weight_sem.at[0]),
        pltpu.make_async_copy(
            w_gate.at[:, 0:first], pair_buf.at[0:width, :], weight_sem.at[1]
        ),
        pltpu.make_async_copy(
            w_up.at[:, 0:first], pair_buf.at[width : 2 * width, :], weight_sem.at[2]
        ),
        pltpu.make_async_copy(
            w_gate.at[:, first:hidden_width],
            pair_buf.at[2 * width : 3 * width, 0:second],
            weight_sem.at[3],
        ),
        pltpu.make_async_copy(
            w_up.at[:, first:hidden_width],
            pair_buf.at[3 * width : 4 * width, 0:second],
            weight_sem.at[4],
        ),
        pltpu.make_async_copy(w_down, down_buf, weight_sem.at[5]),
    ]

    small_copies = [
        pltpu.make_async_copy(source, target, small_sem.at[i])
        for i, (source, target) in enumerate(
            (
                (queries_in, queries),
                (lengths_in, lengths),
                (residual_in, residual),
                (gain_in, gain),
            )
        )
    ]

    barrier = pltpu.get_barrier_semaphore()
    for other in ctx_others:
        pl.semaphore_signal(barrier, inc=1, device_id={"ctx": other}, device_id_type=MESH)
    for other in head_others:
        pl.semaphore_signal(barrier, inc=1, device_id={"head": other}, device_id_type=MESH)

    def fetch(c, _):
        key_copy(c).start()
        value_copy(c).start()
        return 0

    small_copies[0].start()
    lax.fori_loop(0, early, fetch, 0)

    def exchange(axis, me, others, send_sems, recv_sems, phase, source, slots):
        def one(other, mine):
            return pltpu.make_async_remote_copy(
                src_ref=source(other),
                dst_ref=slots.at[mine],
                send_sem=send_sems.at[phase, other],
                recv_sem=recv_sems.at[phase, mine],
                device_id={axis: other},
                device_id_type=MESH,
            )

        def start():
            for other in others:
                one(other, me).start()

        def arrive():
            for other in reversed(others):
                one(other, other).wait_recv()

        def sent():
            for other in others:
                one(other, me).wait_send()

        return start, arrive, sent

    over_ctx = functools.partial(exchange, "ctx", ctx, ctx_others, ctx_send, ctx_recv)
    over_head = functools.partial(exchange, "head", head, head_others, head_send, head_recv)

    small_copies[0].wait()
    own = queries[...].astype(F32)
    for g in range(GROUPS):
        query_row[pl.ds(g, 4, stride=GROUPS), :] = own[:, g * HEAD : (g + 1) * HEAD]
    query_send[...] = query_row[...].astype(BF16)
    query_all[ctx] = query_send[...]

    pl.semaphore_wait(barrier, ctxs - 1 + heads - 1)
    q_start, q_arrive, q_sent = over_ctx(0, lambda other: query_send, query_all)
    q_start()
    for copy in small_copies[1:]:
        copy.start()
    lax.fori_loop(early, turns, fetch, 0)
    for copy in weight_copies:
        copy.start()
    for copy in small_copies[1:]:
        copy.wait()

    visible[...] = jnp.full(visible.shape, 2**30, jnp.int32)
    visible[0:1, 0:batch] = lengths[...] - offsets[0]
    high[...] = jnp.full(high.shape, -3e38, F32)
    total[...] = jnp.zeros(total.shape, F32)
    acc[...] = jnp.zeros(acc.shape, F32)
    row_of = lax.broadcasted_iota(jnp.int32, (rows, LANES), 0) // GROUPS
    column = lax.broadcasted_iota(jnp.int32, (rows, LANES), 1)
    query_wide[:, HEAD : HEAD + LANES] = jnp.where(row_of == column, HIDDEN_SCORE, 0.0).astype(BF16)
    tall = 16 * ctxs
    spread_buf[...] = jnp.where(
        lax.broadcasted_iota(jnp.int32, (tall, batch), 0) // 16 * 4
        + lax.broadcasted_iota(jnp.int32, (tall, batch), 0) % 4
        == lax.broadcasted_iota(jnp.int32, (tall, batch), 1),
        1.0,
        0.0,
    ).astype(BF16)
    q_arrive()
    query_wide[:, 0:HEAD] = query_all[...].reshape(rows, HEAD)

    def scores(c):
        part = pl.ds(pl.multiple_of(c * block, block), block)
        slot = lax.broadcasted_iota(jnp.int32, (block, LANES), 0)
        beyond = jnp.where(slot >= visible[0:1, :] - c * block, 1.0, 0.0).astype(BF16)
        return dot_across(
            jnp.concatenate([key_buf[part, :], beyond], axis=1), query_wide[...]
        )

    def absorb(c, slot):
        part = pl.ds(pl.multiple_of(c * block, block), block)
        s = score_buf[slot]
        old = high[0:1, :]
        new = jnp.maximum(old, jnp.max(s, axis=0, keepdims=True))
        weights = jnp.exp2((s - new) * base).astype(BF16)
        rescale = jnp.exp2((old - new) * base)
        high[...] = jnp.broadcast_to(new, high.shape)
        upright = jnp.concatenate(
            [value_buf[part, :].T, jnp.ones((16, block), BF16)], axis=0
        )
        update = dot(upright, weights)
        acc[...] = acc[...] * rescale + update[0:HEAD]
        total[...] = total[...] * rescale + update[HEAD : HEAD + 8]

    key_copy(0).wait()
    score_buf[0] = scores(0)

    def visit(i, _):
        c = 2 * i
        key_copy(c + 1).wait()
        value_copy(c).wait()
        key_copy(c + 2).wait()
        value_copy(c + 1).wait()
        score_buf[1] = scores(c + 1)
        absorb(c, 0)
        score_buf[0] = scores(c + 2)
        absorb(c + 1, 1)
        return 0

    lax.fori_loop(0, turns // 2 - 1, visit, 0)
    key_copy(turns - 1).wait()
    value_copy(turns - 2).wait()
    value_copy(turns - 1).wait()
    score_buf[1] = scores(turns - 1)
    absorb(turns - 2, 0)
    absorb(turns - 1, 1)

    high_row = high[0:1, :]
    total_row = total[0:1, :]
    part_send[:, 0:32, :] = (
        (acc[...] / total_row).astype(BF16).T.reshape(ctxs, 32, HEAD)
    )

    def piece(v):
        return v.astype(BF16).astype(F32)

    h1 = piece(high_row)
    h2 = piece(high_row - h1)
    h3 = piece(high_row - h1 - h2)
    t1 = piece(total_row)
    t2 = piece(total_row - t1)
    index = lax.broadcasted_iota(jnp.int32, (16, rows), 0)
    stats = jnp.zeros((16, rows), F32)
    for k, v in enumerate((h1, h2, h3, t1, t2)):
        stats = jnp.where(index == k, v, stats)
    stats = stats.astype(BF16)
    for i in range(ctxs):
        at = i // 4 * LANES
        part_send[i, 32:48, :] = stats[:, at : at + LANES]
    part_recv[ctx] = part_send[ctx]
    p_start, p_arrive, p_sent = over_ctx(1, lambda other: part_send.at[other], part_recv)
    p_start()
    q_sent()
    p_arrive()

    tops = []
    sums = []
    for i in range(ctxs):
        tile = part_recv[i, 32:48, :].astype(F32)
        tops.append(tile[0:1] + tile[1:2] + tile[2:3])
        sums.append(tile[3:4] + tile[4:5])
    tops = jnp.concatenate(tops, axis=0)
    sums = jnp.concatenate(sums, axis=0)
    shares = sums * jnp.exp2((tops - jnp.max(tops, axis=0, keepdims=True)) * base)
    shares = shares / jnp.sum(shares, axis=0, keepdims=True)
    square_tile[...] = jnp.zeros(square_tile.shape, F32)
    square_tile[0:ctxs, :] = shares
    square_tile[...] = square_tile[...].T
    mine = square_tile[pl.ds(pl.multiple_of(lax.rem(ctx, 4) * 32, 32), 32), :]
    merged = jnp.zeros((32, HEAD), F32)
    for i in range(ctxs):
        merged = merged + part_recv[i, 0:32, :].astype(F32) * mine[:, i : i + 1]
    rows_send[...] = merged.astype(BF16)
    rows_all[ctx] = rows_send[...]
    r_start, r_arrive, r_sent = over_ctx(2, lambda other: rows_send, rows_all)
    r_start()
    rows_f32[...] = rows_send[...].astype(F32)
    for g in range(GROUPS):
        attended[:, g * HEAD : (g + 1) * HEAD] = rows_f32[pl.ds(g, 4, stride=GROUPS), :].astype(
            BF16
        )
    p_sent()
    weight_copies[0].wait()
    r_arrive()

    kept = width - 64
    quarter = batch // 4

    def pack(v):
        parts = [v[i * quarter : (i + 1) * quarter, kept:width] for i in range(4)]
        return jnp.concatenate([v[:, 0:kept], jnp.concatenate(parts, axis=1)], axis=0)

    def unpack(v):
        parts = [v[batch : batch + quarter, i * 64 : (i + 1) * 64] for i in range(4)]
        return jnp.concatenate([v[0:batch], jnp.concatenate(parts, axis=0)], axis=1)

    wide_f32[...] = rows_all[...].astype(F32).reshape(rows, HEAD)
    projected = jnp.zeros((batch, width), F32)
    for g in range(GROUPS):
        lines = wide_f32[pl.ds(g, batch, stride=GROUPS), :].astype(BF16)
        projected = projected + dot_across(lines, wo_buf[:, g * HEAD : (g + 1) * HEAD])
    proj_all[head] = pack(projected).astype(BF16)
    d_start, d_arrive, d_sent = over_head(0, lambda other: proj_all.at[head], proj_all)
    d_start()
    r_sent()
    d_arrive()

    mixed = proj_all[0].astype(F32)
    for i in range(1, heads):
        mixed = mixed + proj_all[i].astype(F32)
    combined = residual[...].astype(F32) + unpack(mixed)
    stream[...] = combined.astype(BF16)
    squares = jnp.sum(combined * combined, axis=1, keepdims=True)
    normed = (combined * gain[...].reshape(1, width)).astype(BF16)

    spread = spread_buf[...]
    copies = dot(spread, normed)
    which = lax.broadcasted_iota(jnp.int32, (tall, width), 0) % 16 // 4
    for k in range(4):
        lhs[:, k * width : (k + 1) * width] = jnp.where(which == k, copies, 0.0).astype(BF16)
    s1 = squares.astype(BF16).astype(F32)
    s2 = squares - s1
    lane = lax.broadcasted_iota(jnp.int32, (batch, LANES), 1)
    marks = jnp.where(lane == 0, s1, jnp.where(lane == 1, s2, 0.0)).astype(BF16)
    marks = dot(spread, marks)
    for copy in weight_copies[1:5]:
        copy.wait()
    full = lhs[...]

    gates = []
    hiddens = []
    for k, (gate_send, gate_recv, hidden_send, hidden_all) in enumerate(pieces):
        low, top = cuts[k]
        for at in range(low, min(top, second), 256):
            wide = min(256, min(top, second) - at)
            gate_send[:, :, at - low : at - low + wide] = (
                dot(full, pair_buf[:, at : at + wide]).astype(BF16).reshape(ctxs, 16, wide)
            )
        if top > second:
            gate_send[:, :, second - low : top - low] = (
                jnp.where(
                    lax.broadcasted_iota(jnp.int32, (tall, LANES), 0) % 16 < 8,
                    dot(full[:, 0 : 2 * width], pair_buf[0 : 2 * width, second:top]),
                    marks,
                )
                .astype(BF16)
                .reshape(ctxs, 16, top - second)
            )
        gate_recv[ctx] = gate_send[ctx]
        gates.append(over_ctx(3 + k, lambda other, sent=gate_send: sent.at[other], gate_recv))
        gates[k][0]()
    d_sent()

    def gated(v):
        return v / (1.0 + jnp.exp(-v)) * pltpu.roll(v, 4, 0)

    for k, (gate_send, gate_recv, hidden_send, hidden_all) in enumerate(pieces):
        low, top = cuts[k]
        gates[k][1]()
        summed = gate_recv[0].astype(F32)
        for i in range(1, ctxs):
            summed = summed + gate_recv[i].astype(F32)
        if k == 0:
            square_total = jnp.sum(summed[8:16, second - low : top - low], axis=1, keepdims=True)
            scale = lax.rsqrt(square_total / model + EPSILON)
            scale = jnp.concatenate([scale, scale], axis=0)
        scaled = summed[:, 0 : top - low] * scale
        upper = gated(scaled[0:8])
        lower = gated(scaled[8:16])
        index = lax.broadcasted_iota(jnp.int32, upper.shape, 0)
        hidden_send[...] = jnp.where(index < 4, upper, pltpu.roll(lower, 4, 0)).astype(BF16)
        hidden_all[ctx] = hidden_send[...]
        hiddens.append(
            over_ctx(3 + len(pieces) + k, lambda other, sent=hidden_send: sent, hidden_all)
        )
        hiddens[k][0]()
    weight_copies[5].wait()
    one = jnp.zeros((8 * ctxs, width), F32)
    two = jnp.zeros((8 * ctxs, width), F32)
    for k, (gate_send, gate_recv, hidden_send, hidden_all) in enumerate(pieces):
        low, top = cuts[k]
        hiddens[k][1]()
        hidden = hidden_all[...].astype(F32).reshape(8 * ctxs, top - low).astype(BF16)
        one = one + dot_across(hidden, down_buf[:, low:top])
        rest = min(top, second) - low
        two = two + dot_across(hidden[:, 0:rest], down_buf[:, first + low : first + low + rest])
    both = one + pltpu.roll(two, 8 * ctxs - 4, 0)
    index = lax.broadcasted_iota(jnp.int32, (8, width), 0)
    for i in range(heads):
        down_send[i] = jnp.where(
            index < 4,
            both[16 * i : 16 * i + 8],
            pltpu.roll(both[16 * i + 8 : 16 * i + 16], 4, 0),
        ).astype(BF16)
    down_recv[head] = down_send[head]
    f_start, f_arrive, f_sent = over_head(1, lambda other: down_send.at[other], down_recv)
    f_start()
    for k in range(len(pieces)):
        gates[k][2]()
        hiddens[k][2]()
    f_arrive()
    result = down_recv[0].astype(F32)
    for i in range(1, heads):
        result = result + down_recv[i].astype(F32)
    ffn_out[...] = result.astype(BF16)
    f_sent()


def hand_over(a_in, b_in, c_in, a, b, c, sem):
    copies = [
        pltpu.make_async_copy(source, target, sem.at[i])
        for i, (source, target) in enumerate(((a_in, a), (b_in, b), (c_in, c)))
    ]
    for copy in copies:
        copy.start()
    for copy in copies:
        copy.wait()


def local(
    ctxs,
    heads,
    block,
    queries,
    keys,
    values,
    offsets,
    lengths,
    residual,
    wo,
    norm_gain,
    w_gate,
    w_up,
    w_down,
):
    span = keys.shape[0]
    batch, width = residual.shape
    rows = batch * GROUPS
    hidden_width = w_gate.shape[1]
    first = (hidden_width // LANES + 1) // 2 * LANES
    cuts = cuts_of(first)
    slabs = []
    for k in range(PIECES):
        wide = cuts[k][1] - cuts[k][0]
        slabs += [
            pltpu.VMEM((ctxs, 16, wide), BF16),
            pltpu.VMEM((ctxs, 16, wide), BF16),
            pltpu.VMEM((8, wide), BF16),
            pltpu.VMEM((ctxs, 8, wide), BF16),
        ]
    sizes = (ctxs, heads, span, block, width, width * ctxs)
    vmem = pl.BlockSpec(memory_space=pltpu.VMEM)
    hbm = pl.BlockSpec(memory_space=pltpu.HBM)
    smem = pl.BlockSpec(memory_space=pltpu.SMEM)
    free = pl.BlockSpec(memory_space=pl.ANY)
    outs = (
        jax.ShapeDtypeStruct(queries.shape, BF16),
        jax.ShapeDtypeStruct((batch, width), BF16),
        jax.ShapeDtypeStruct((batch // heads, width), BF16),
    )
    results = pl.pallas_call(
        functools.partial(kernel, sizes),
        out_shape=tuple(pltpu.VMEM(o.shape, o.dtype) for o in outs),
        in_specs=[smem] + [hbm] * 10,
        out_specs=(vmem, vmem, vmem),
        scratch_shapes=[
            pltpu.VMEM(queries.shape, BF16),
            pltpu.VMEM((1, batch), jnp.int32),
            pltpu.VMEM(residual.shape, BF16),
            pltpu.VMEM((width,), F32),
            pltpu.VMEM((span, HEAD), BF16),
            pltpu.VMEM((span, HEAD), BF16),
            pltpu.VMEM((width, rows * HEAD // batch), BF16),
            pltpu.VMEM((4 * width, first), BF16),
            pltpu.VMEM((width, hidden_width), BF16),
            pltpu.VMEM((8, LANES), jnp.int32),
            pltpu.VMEM((32, HEAD), F32),
            pltpu.VMEM((32, HEAD), BF16),
            pltpu.VMEM((ctxs, 32, HEAD), BF16),
            pltpu.VMEM((rows, HEAD + LANES), BF16),
            pltpu.VMEM((2, block, rows), F32),
            pltpu.VMEM((8, rows), F32),
            pltpu.VMEM((8, rows), F32),
            pltpu.VMEM((HEAD, rows), F32),
            pltpu.VMEM((ctxs, 48, HEAD), BF16),
            pltpu.VMEM((ctxs, 48, HEAD), BF16),
            pltpu.VMEM((32, HEAD), F32),
            pltpu.VMEM((32, HEAD), BF16),
            pltpu.VMEM((ctxs, 32, HEAD), BF16),
            pltpu.VMEM((rows, HEAD), F32),
            pltpu.VMEM((heads, batch + batch // 4, 256), BF16),
            pltpu.VMEM((LANES, LANES), F32),
            pltpu.VMEM((16 * ctxs, 4 * width), BF16),
            pltpu.VMEM((16 * ctxs, batch), BF16),
            pltpu.VMEM((heads, 8, width), BF16),
            pltpu.VMEM((heads, 8, width), BF16),
            pltpu.SemaphoreType.DMA((2, span // block)),
            pltpu.SemaphoreType.DMA((6,)),
            pltpu.SemaphoreType.DMA((4,)),
            pltpu.SemaphoreType.DMA((3 + 2 * PIECES, ctxs)),
            pltpu.SemaphoreType.DMA((3 + 2 * PIECES, ctxs)),
            pltpu.SemaphoreType.DMA((2, heads)),
            pltpu.SemaphoreType.DMA((2, heads)),
        ]
        + slabs,
        compiler_params=pltpu.CompilerParams(
            collective_id=0, has_side_effects=True, vmem_limit_bytes=GRANT
        ),
        name="layer",
    )(
        offsets,
        *(
            pltpu.with_memory_space_constraint(x, pltpu.HBM)
            for x in (
                queries,
                lengths.reshape(1, batch),
                residual,
                norm_gain,
                keys.reshape(span, HEAD),
                values.reshape(span, HEAD),
                wo.T,
                w_gate,
                w_up,
                w_down.T,
            )
        )
    )
    return pl.pallas_call(
        hand_over,
        out_shape=outs,
        in_specs=[free] * 3,
        out_specs=(free,) * 3,
        scratch_shapes=[pltpu.SemaphoreType.DMA((3,))],
        compiler_params=pltpu.CompilerParams(vmem_limit_bytes=1024 * 1024),
        name="hand_over",
    )(*results)


def solution(mesh, block=4096):
    return jax.shard_map(
        functools.partial(local, mesh.shape["ctx"], mesh.shape["head"], block),
        mesh=mesh,
        in_specs=(
            P("ctx", "head"),
            P("ctx", "head", None),
            P("ctx", "head", None),
            P("ctx"),
            P(),
            P(None, "ctx"),
            P("head", "ctx"),
            P("ctx"),
            P("ctx", "head"),
            P("ctx", "head"),
            P("head", "ctx"),
        ),
        out_specs=(P("ctx", "head"), P(None, "ctx"), P("head", "ctx")),
        check_vma=False,
    )
```
